32 devices in a mesh: row: 8 (over z, core), col: 4 (over y, x).
Axes of the slice: x: 2, y: 2, z: 4, core: 2. Of those that a mesh axis runs over, the one named last changes fastest.
Arguments:
- context: bfloat16 [128, 16384], P('row', 'col'), may hold values from -6 to 6
- out_weight: bfloat16 [16384, 16384], P('col', 'row'), may hold values from -0.046875 to 0.046875
- residual: bfloat16 [128, 16384], P('col', 'row'), may hold values from -80 to 80
- teacher_gain: float32 [16384], replicated, may hold values from 0.5 to 1.5
- student_hidden: bfloat16 [128, 4096], P(('row', 'col')), may hold values from -6 to 6
- student_gain: float32 [4096], replicated, may hold values from 0.5 to 1.5
- projector: bfloat16 [4096, 16384], P(None, ('row', 'col')), may hold values from -0.09375 to 0.09375
Outputs:
- grad_proj: float32 [4096, 16384], P(None, ('row', 'col'))
- grad_gain: float32 [4096], replicated
- loss: float32 [], replicated
The draws below stay inside these ranges and needn't reach their ends.
All inputs are finite; a program needn't handle non-finite values.
Results may differ from the reference program's by a relative error of at most 0.0065.
Values may be sent and summed in bfloat16 or wider, within the bound.
A program may use at most 64 MiB of HBM per device.

```python
import math
import jax
import jax.numpy as jnp
from jax import lax

D_T = 16384
D_S = 4096
TOKENS = 128


def draw_residual(key, part):
    keys = jax.random.split(key, 3)
    ramp = jnp.exp(jnp.linspace(0.0, math.log(3.0), D_T))
    column = ramp * jnp.exp(jax.random.uniform(keys[1], (D_T,), minval=0.0, maxval=math.log(2.0)))
    rowwise = jnp.exp(jax.random.uniform(keys[2], (TOKENS, 1), minval=0.0, maxval=math.log(4.0)))
    base = jnp.clip(jax.random.normal(keys[0], (TOKENS, D_T)), -6.0, 6.0)
    return (base * rowwise * column * 0.5).astype(jnp.bfloat16)


def block_scale(own_key, dims, cuts, smallest, largest):
    level = 1.0
    for dim, blocks in cuts:
        heights = jax.random.uniform(jax.random.fold_in(jax.random.fold_in(own_key, 6), dim), (blocks,), jnp.float32, smallest / len(cuts), largest / len(cuts))
        level = level * jnp.repeat(jnp.exp(heights), dims[dim] // blocks).reshape((-1,) + (1,) * (len(dims) - 1 - dim))
    return level


def normal_values(stream_key, dims, deviation, bound, pieces=(), held_as=jnp.bfloat16):
    result = deviation * jax.random.normal(stream_key, dims, jnp.float32)
    if pieces:
        result = result * block_scale(stream_key, dims, pieces, -0.22, 0.18)
    return jnp.clip(result, -bound, bound).astype(held_as)


def setup_inputs(seed: int = 0) -> dict:
    seeds = jax.random.split(jax.random.key(seed), 8)
    return {
        "context": normal_values(seeds[0], (TOKENS, D_T), 1.0, 6.0, ((0, 8), (1, 4))),
        "out_weight": normal_values(seeds[1], (D_T, D_T), D_T ** -0.5, 0.046875, ((0, 4), (1, 8))),
        "residual": draw_residual(jax.random.fold_in(seeds[7], 71), 0),
        "teacher_gain": jnp.clip(jax.random.uniform(seeds[3], (D_T,), jnp.float32, 0.5, 1.5), 0.5, 1.5),
        "student_hidden": normal_values(seeds[4], (TOKENS, D_S), 1.0, 6.0, ((0, 32),)),
        "student_gain": jnp.clip(jax.random.uniform(seeds[5], (D_S,), jnp.float32, 0.5, 1.5), 0.5, 1.5),
        "projector": normal_values(seeds[6], (D_S, D_T), D_S ** -0.5, 0.09375, ((1, 32),)),
    }


norm_eps = 1e-05

def reference(context, out_weight, residual, teacher_gain, student_hidden, student_gain, projector):
    teacher_sum = jnp.dot(context, out_weight, preferred_element_type=jnp.float32) + residual.astype(jnp.float32)
    squares = lax.optimization_barrier(jnp.mean(teacher_sum * teacher_sum, axis=1, keepdims=True))
    target = (teacher_sum * lax.rsqrt(squares + norm_eps) * teacher_gain).astype(jnp.bfloat16)
    widened = student_hidden.astype(jnp.float32)
    normed = widened * lax.rsqrt(lax.optimization_barrier(jnp.mean(widened * widened, axis=1, keepdims=True)) + norm_eps)
    student_out = (normed * student_gain).astype(jnp.bfloat16)
    predicted = jnp.dot(student_out, projector, preferred_element_type=jnp.float32)
    difference = predicted - target.astype(jnp.float32)
    loss = jnp.sum(difference * difference) / (TOKENS * D_T)
    error_term = (difference * (1.0 / 64.0)).astype(jnp.bfloat16)
    grad_proj = jnp.dot(student_out.T, error_term, preferred_element_type=jnp.float32)
    grad_normed = jnp.dot(error_term, projector.T, preferred_element_type=jnp.float32)
    grad_gain = lax.optimization_barrier(jnp.sum(grad_normed * normed, axis=0))
    return (grad_proj, grad_gain, loss)
```

```python
import functools

import jax
import jax.numpy as jnp
from jax import lax
from jax.experimental import pallas as pl
from jax.experimental.pallas import tpu as pltpu
from jax.sharding import PartitionSpec as P

norm_eps = 1e-05
LANES = 128
CHUNKS = 4
MESH = pl.DeviceIdType.MESH


def to_row(column):
    return jnp.transpose(jnp.broadcast_to(column, (LANES, LANES)))[0:1, :]


def to_column(row):
    return jnp.transpose(jnp.broadcast_to(row, (LANES, LANES)))[:, 0:1]


def body(
    n_row, n_col,
    context, weight, residual, teacher_gain, hidden, student_gain, projector,
    student_out, error_out, gain_out, loss_out,
    ctx, w, proj, acc, part_out, part_in, res, hid, wide, inverse, sgain, tgain,
    predicted, total, sq_out, sq_in, gp, gp_in, gg_out, gg,
    local_sem, w_sem, ctx_send, ctx_recv, hid_chain, hid_partner, hid_col, hid_recv,
    col_send, col_recv, all_send, all_recv,
):
    devices = n_row * n_col
    chips = n_row // 2
    r, c = lax.axis_index("row"), lax.axis_index("col")
    me = r * n_col + c
    p, core = r // 2, r % 2
    tok = context.shape[0]
    features = context.shape[1]
    chunk = features // CHUNKS
    tokens = tok * n_row
    width = proj.shape[1]
    res_rows = residual.shape[0]
    hid_rows = hidden.shape[0]
    d_s = hidden.shape[1]
    d_t = width * devices
    segments = gain_out.shape[0]
    repeat = devices // segments

    def rows_of(row):
        return pl.ds(pl.multiple_of(row * tok, tok), tok)

    def row_of(pos):
        return pos * 2 + core

    own = [
        pltpu.make_async_copy(context, ctx.at[rows_of(r), :], local_sem.at[0]),
        pltpu.make_async_copy(hidden, hid.at[me], local_sem.at[1]),
        pltpu.make_async_copy(
            residual.at[:, pl.ds(pl.multiple_of(c * width, width), width)],
            res.at[pl.ds(pl.multiple_of(c * res_rows, res_rows), res_rows), :],
            local_sem.at[2],
        ),
    ]
    for copy in own:
        copy.start()

    def w_copy(k):
        part = pl.ds(k * chunk, chunk)
        return pltpu.make_async_copy(weight.at[part, :], w.at[part, :], w_sem.at[k])

    for k in range(CHUNKS):
        w_copy(k).start()
    proj_copy = pltpu.make_async_copy(projector, proj, local_sem.at[3])
    proj_copy.start()

    barrier = pltpu.get_barrier_semaphore()

    def greet(i, _):
        d = (me + 1 + i) % devices
        pl.semaphore_signal(
            barrier, inc=1, device_id=(d // n_col, d % n_col), device_id_type=MESH
        )
        return 0

    lax.fori_loop(0, devices - 1, greet, 0)
    pl.semaphore_wait(barrier, devices - 1)

    up, down, partner = (r + 2, c), (r - 2, c), (r + 1 - 2 * core, c)
    targets = {0: up, 1: down, 2: partner}

    def ctx_copy(pos, k, way, first=False):
        row = row_of(pos)
        cols = pl.ds(k * chunk, chunk)
        there = ctx.at[rows_of(row), cols]
        return pltpu.make_async_remote_copy(
            src_ref=context.at[:, cols] if first else there,
            dst_ref=there,
            send_sem=ctx_send.at[way, pos, k],
            recv_sem=ctx_recv.at[row, k],
            device_id=targets[way],
            device_id_type=MESH,
        )

    def hid_copy(row, col, device, send_sem, first=False):
        slot = row * n_col + col
        return pltpu.make_async_remote_copy(
            src_ref=hidden if first else hid.at[slot],
            dst_ref=hid.at[slot],
            send_sem=send_sem,
            recv_sem=hid_recv.at[slot],
            device_id=device,
            device_id_type=MESH,
        )

    def hid_way(pos, way, first=False):
        return hid_copy(row_of(pos), c, targets[way], hid_chain.at[way, pos], first)

    def hid_side(pos, i, first=False):
        return hid_copy(row_of(pos), c, (r, (c + 1 + i) % n_col), hid_col.at[i, pos], first)

    def hid_cross(pos, i):
        col = (c + 1 + i) % n_col
        return hid_copy(row_of(pos), col, partner, hid_partner.at[i, pos])

    def res_copy(i):
        j = (c + 1 + i) % n_col
        return pltpu.make_async_remote_copy(
            src_ref=residual.at[:, pl.ds(pl.multiple_of(j * width, width), width)],
            dst_ref=res.at[pl.ds(pl.multiple_of(c * res_rows, res_rows), res_rows), :],
            send_sem=col_send.at[0, i],
            recv_sem=col_recv.at[0, c],
            device_id=(r, j),
            device_id_type=MESH,
        )

    has_up, has_down = p < chips - 1, p > 0

    def each_way(guard_up, guard_down, fn):
        @pl.when(guard_up)
        def _():
            fn(0)

        @pl.when(guard_down)
        def _():
            fn(1)

    each_way(has_up, has_down, lambda way: hid_way(p, way, True).start())
    for k in range(CHUNKS):
        each_way(has_up, has_down, lambda way: ctx_copy(p, k, way, True).start())
        ctx_copy(p, k, 2, True).start()
    for i in range(n_col - 1):
        hid_side(p, i, True).start()
        res_copy(i).start()
    hid_way(p, 2, True).start()

    def arrive_hid(pos, way, onward):
        hid_way(pos, way).wait_recv()

        @pl.when(onward)
        def _():
            hid_way(pos, way).start()

        hid_way(pos, 2).start()
        for i in range(n_col - 1):
            hid_side(pos, i).start()

    def arrive_ctx(pos, k, way, onward):
        ctx_copy(pos, k, way).wait_recv()

        @pl.when(onward)
        def _():
            ctx_copy(pos, k, way).start()

        ctx_copy(pos, k, 2).start()

    def both(distance, fn):
        @pl.when(p >= distance)
        def _():
            fn(p - distance, 0, has_up)

        @pl.when(p + distance < chips)
        def _():
            fn(p + distance, 1, has_down)

    for distance in range(1, chips):
        both(distance, arrive_hid)
        if distance < chips - 1:
            for k in range(CHUNKS):
                both(distance, lambda pos, way, on: arrive_ctx(pos, k, way, on))

    own[0].wait()
    partner_row = r + 1 - 2 * core

    def product(j, k):
        cols = pl.ds(pl.multiple_of(j * width, width), width)
        return jnp.dot(
            ctx[:, k * chunk:(k + 1) * chunk],
            w[k * chunk:(k + 1) * chunk, cols],
            preferred_element_type=jnp.float32,
        )

    def part_copy(i):
        j = (c + 1 + i) % n_col
        return pltpu.make_async_remote_copy(
            src_ref=part_out.at[i],
            dst_ref=part_in.at[c],
            send_sem=col_send.at[1, i],
            recv_sem=col_recv.at[1, c],
            device_id=(r, j),
            device_id_type=MESH,
        )

    for k in range(CHUNKS):
        if chips > 1:
            both(chips - 1, lambda pos, way, on: arrive_ctx(pos, k, way, on))
        for pos in range(chips):
            row = pos * 2 + 1 - core
            there = ctx.at[rows_of(row), pl.ds(k * chunk, chunk)]
            pltpu.make_async_remote_copy(
                src_ref=there, dst_ref=there, send_sem=ctx_send.at[2, pos, k],
                recv_sem=ctx_recv.at[row, k], device_id=partner, device_id_type=MESH,
            ).wait_recv()
        w_copy(k).wait()
        if k < CHUNKS - 1:
            def step(j, _, k=k):
                if k == 0:
                    acc[j] = product(j, k)
                else:
                    acc[j] += product(j, k)
                return 0

            lax.fori_loop(0, n_col, step, 0)
        else:
            def last(i, _):
                j = (c + 1 + i) % n_col
                part_out[i] = (acc[j] + product(j, CHUNKS - 1)).astype(jnp.bfloat16)
                part_copy(i).start()
                return 0

            lax.fori_loop(0, n_col - 1, last, 0)
            acc[c] = acc[c] + product(c, CHUNKS - 1)

    for pos in range(chips):
        for i in range(n_col - 1):
            j = (c + 1 + i) % n_col
            hid_copy(row_of(pos), j, (r, j), hid_col.at[i, pos]).wait_recv()
            hid_cross(pos, i).start()
    for j in range(student_gain.shape[0]):
        sgain[:, j * LANES:(j + 1) * LANES] = student_gain[j:j + 1, :]
    gain_rows = width // LANES
    for j in range(gain_rows):
        tgain[:, j * LANES:(j + 1) * LANES] = teacher_gain[pl.ds(me * gain_rows + j, 1), :]
    for pos in range(chips):
        for j in range(n_col):
            hid_copy(pos * 2 + 1 - core, j, partner, hid_chain.at[2, pos]).wait_recv()
    own[1].wait()

    group = 8 // hid_rows if hid_rows < 8 else 1

    def widen(s, _):
        wide_rows = pl.ds(pl.multiple_of(s * group * hid_rows, 8), group * hid_rows)
        wide[wide_rows, :] = jnp.concatenate(
            [hid[s * group + i].astype(jnp.float32) for i in range(group)], axis=0
        )
        return 0

    lax.fori_loop(0, devices // group, widen, 0)

    tile = 16

    def normalize(t, _):
        rows = pl.ds(pl.multiple_of(t * tile, tile), tile)
        x = wide[rows, :]
        normed = x * lax.rsqrt(jnp.mean(x * x, axis=1, keepdims=True) + norm_eps)
        wide[rows, :] = normed
        student_out[rows, :] = (normed * sgain[...]).astype(jnp.bfloat16)
        return 0

    lax.fori_loop(0, tokens // tile, normalize, 0)
    proj_copy.wait()
    predicted[...] = jnp.dot(student_out[...], proj[...], preferred_element_type=jnp.float32)

    own[2].wait()
    for i in range(n_col - 1):
        j = (c + 1 + i) % n_col
        pltpu.make_async_remote_copy(
            src_ref=part_out.at[i], dst_ref=part_in.at[j], send_sem=col_send.at[1, i],
            recv_sem=col_recv.at[1, j], device_id=(r, j), device_id_type=MESH,
        ).wait_recv()
        rows = res.at[pl.ds(pl.multiple_of(j * res_rows, res_rows), res_rows), :]
        pltpu.make_async_remote_copy(
            src_ref=rows, dst_ref=rows, send_sem=col_send.at[0, i],
            recv_sem=col_recv.at[0, j], device_id=(r, j), device_id_type=MESH,
        ).wait_recv()
    summed = acc[c] + res[...].astype(jnp.float32)
    for i in range(n_col - 1):
        summed = summed + part_in[(c + 1 + i) % n_col].astype(jnp.float32)
    total[...] = summed
    squares = jnp.sum(summed * summed, axis=1, keepdims=True)
    for b in range(tokens // LANES):
        lanes = slice(b * LANES, (b + 1) * LANES)
        row = to_row(squares[lanes, :])
        sq_out[:, lanes] = row
        sq_in[me, :, lanes] = row

    def to_all(stage, src, dst):
        def copy(i):
            d = (me + 1 + i) % devices
            return pltpu.make_async_remote_copy(
                src_ref=src(d), dst_ref=dst.at[me],
                send_sem=all_send.at[stage], recv_sem=all_recv.at[stage],
                device_id=(d // n_col, d % n_col), device_id_type=MESH,
            )

        def send(i, _):
            copy(i).start()
            return 0

        lax.fori_loop(0, devices - 1, send, 0)

    def wait_all(sem, stage, dst):
        view = dst.at[pl.ds(0, devices - 1)]
        pltpu.make_async_copy(view, view, sem.at[stage]).wait()

    to_all(0, lambda d: sq_out, sq_in)
    wait_all(all_recv, 0, sq_in)
    sums = jnp.sum(sq_in[...], axis=0)
    factor = lax.rsqrt(sums / d_t + norm_eps)
    loss_part = jnp.zeros((1, 1), jnp.float32)
    for b in range(tokens // LANES):
        rows = slice(b * LANES, (b + 1) * LANES)
        target = (total[rows, :] * to_column(factor[:, rows]) * tgain[...]).astype(jnp.bfloat16)
        difference = predicted[rows, :] - target.astype(jnp.float32)
        loss_part = loss_part + jnp.sum(difference * difference, keepdims=True)
        error_out[rows, :] = (difference * (1.0 / 64.0)).astype(jnp.bfloat16)

    block = 512

    def gain_step(n, _):
        rows = pl.ds(pl.multiple_of(n * block, block), block)
        grad_normed = lax.dot_general(
            error_out[...], proj[rows, :], (((1,), (1,)), ((), ())),
            preferred_element_type=jnp.float32,
        )
        part = jnp.sum(grad_normed * wide[:, rows], axis=0, keepdims=True)
        for q in range(block // LANES):
            gp[n * (block // LANES) + q, 0:1, :] = part[:, q * LANES:(q + 1) * LANES]
            gp[n * (block // LANES) + q, 1:2, :] = jnp.broadcast_to(loss_part, (1, LANES))
        return 0

    lax.fori_loop(0, d_s // block, gain_step, 0)
    gp_in[me] = gp[me // repeat]
    to_all(1, lambda d: gp.at[d // repeat], gp_in)
    wait_all(all_recv, 1, gp_in)
    both_sums = jnp.sum(gp_in[...], axis=0)
    gg_out[...] = both_sums[0:1, :]
    gg[me] = both_sums[0:1, :]
    to_all(2, lambda d: gg_out, gg)
    loss_out[...] = both_sums[1:2, :] / (tokens * d_t)
    wait_all(all_recv, 2, gg)
    for j in range(segments):
        gain_out[j:j + 1, :] = gg[j * repeat]

    each_way(has_up, has_down, lambda way: hid_way(p, way).wait_send())
    hid_way(p, 2).wait_send()
    for k in range(CHUNKS):
        each_way(has_up, has_down, lambda way: ctx_copy(p, k, way).wait_send())
        ctx_copy(p, k, 2).wait_send()
    for i in range(n_col - 1):
        hid_side(p, i).wait_send()
        res_copy(i).wait_send()
        part_copy(i).wait_send()

    def left(pos, way, onward):
        @pl.when(onward)
        def _():
            hid_way(pos, way).wait_send()
            for k in range(CHUNKS):
                ctx_copy(pos, k, way).wait_send()

        hid_way(pos, 2).wait_send()
        for k in range(CHUNKS):
            ctx_copy(pos, k, 2).wait_send()
        for i in range(n_col - 1):
            hid_side(pos, i).wait_send()

    for distance in range(1, chips):
        both(distance, left)
    for pos in range(chips):
        for i in range(n_col - 1):
            hid_cross(pos, i).wait_send()
    wait_all(all_send, 0, sq_in)
    wait_all(all_send, 1, gp_in)
    wait_all(all_send, 2, gg)


def per_device(
    n_row, n_col,
    context, out_weight, residual, teacher_gain, student_hidden, student_gain, projector,
):
    devices = n_row * n_col
    chips = n_row // 2
    tokens = context.shape[0] * n_row
    d_s, width = projector.shape
    segments = min(devices, d_s // LANES)
    f32, bf16 = jnp.float32, jnp.bfloat16
    anywhere = pl.BlockSpec(memory_space=pl.ANY)
    vmem = pl.BlockSpec(memory_space=pltpu.VMEM)
    dma = pltpu.SemaphoreType.DMA
    student_all, error_term, grad_gain, loss = pl.pallas_call(
        functools.partial(body, n_row, n_col),
        out_shape=(
            jax.ShapeDtypeStruct((tokens, d_s), bf16),
            jax.ShapeDtypeStruct((tokens, width), bf16),
            jax.ShapeDtypeStruct((segments, LANES), f32),
            jax.ShapeDtypeStruct((1, LANES), f32),
        ),
        in_specs=[anywhere, anywhere, anywhere, vmem, anywhere, vmem, anywhere],
        out_specs=(vmem, vmem, vmem, vmem),
        scratch_shapes=[
            pltpu.VMEM((tokens, context.shape[1]), bf16),
            pltpu.VMEM(out_weight.shape, bf16),
            pltpu.VMEM((d_s, width), bf16),
            pltpu.VMEM((n_col, tokens, width), f32),
            pltpu.VMEM((n_col - 1, tokens, width), bf16),
            pltpu.VMEM((n_col, tokens, width), bf16),
            pltpu.VMEM((tokens, width), bf16),
            pltpu.VMEM((devices,) + student_hidden.shape, bf16),
            pltpu.VMEM((tokens, d_s), f32),
            pltpu.VMEM((8, LANES), f32),
            pltpu.VMEM((1, d_s), f32),
            pltpu.VMEM((1, width), f32),
            pltpu.VMEM((tokens, width), f32),
            pltpu.VMEM((tokens, width), f32),
            pltpu.VMEM((1, tokens), f32),
            pltpu.VMEM((devices, 1, tokens), f32),
            pltpu.VMEM((d_s // LANES, 2, LANES), f32),
            pltpu.VMEM((devices, 2, LANES), f32),
            pltpu.VMEM((1, LANES), f32),
            pltpu.VMEM((devices, 1, LANES), f32),
            dma((4,)),
            dma((CHUNKS,)),
            dma((3, chips, CHUNKS)),
            dma((n_row, CHUNKS)),
            dma((3, chips)),
            dma((n_col, chips)),
            dma((n_col, chips)),
            dma((devices,)),
            dma((2, n_col)),
            dma((2, n_col)),
            dma((3,)),
            dma((3,)),
        ],
        compiler_params=pltpu.CompilerParams(
            collective_id=0, has_side_effects=True, vmem_limit_bytes=48 * 1024 * 1024
        ),
    )(
        context, out_weight, residual, teacher_gain.reshape(-1, LANES), student_hidden,
        student_gain.reshape(-1, LANES), projector,
    )
    grad_proj = lax.dot_general(
        student_all, error_term, (((0,), (0,)), ((), ())), preferred_element_type=f32
    )
    return (grad_proj, grad_gain.reshape(-1), loss[0, 0])


def solution(mesh):
    placed = (
        P("row", "col"),
        P("col", "row"),
        P("col", "row"),
        P(),
        P(("row", "col"), None),
        P(),
        P(None, ("row", "col")),
    )
    return jax.shard_map(
        functools.partial(per_device, mesh.shape["row"], mesh.shape["col"]),
        mesh=mesh,
        in_specs=placed,
        out_specs=(P(None, ("row", "col")), P(), P()),
        check_vma=False,
    )
```

```python
import functools

import jax
import jax.numpy as jnp
from jax import lax
from jax.experimental import pallas as pl
from jax.experimental.pallas import tpu as pltpu
from jax.sharding import PartitionSpec as P

norm_eps = 1e-05
LANES = 128
CHUNKS = 4
HIDDEN_AT = 2
AHEAD = 3
MESH = pl.DeviceIdType.MESH


def to_row(column):
    return jnp.transpose(jnp.broadcast_to(column, (LANES, LANES)))[0:1, :]


def to_column(row):
    return jnp.transpose(jnp.broadcast_to(row, (LANES, LANES)))[:, 0:1]


def body(
    n_row, n_col,
    context, weight, residual, teacher_gain, hidden, student_gain, projector,
    student_out, error_out, gain_out, loss_out,
    student, error, ctx, w, proj, acc, part_out, part_in, res, hid, wide, sgain, tgain,
    predicted, total, sq_out, sq_in, gp, gp_in, gg_out, gg,
    local_sem, w_sem, ctx_send, ctx_recv, hid_chain, hid_partner, hid_col, hid_recv,
    col_send, col_recv, all_send, all_recv,
):
    devices = n_row * n_col
    chips = n_row // 2
    r, c = lax.axis_index("row"), lax.axis_index("col")
    me = r * n_col + c
    p, core = r // 2, r % 2
    tok = context.shape[0]
    features = context.shape[1]
    chunk = features // CHUNKS
    tokens = tok * n_row
    width = proj.shape[1]
    res_rows = residual.shape[0]
    hid_rows = hidden.shape[0]
    d_s = hidden.shape[1]
    d_t = width * devices
    segments = gain_out.shape[0]
    repeat = devices // segments

    def rows_of(row):
        return pl.ds(pl.multiple_of(row * tok, tok), tok)

    def row_of(pos):
        return pos * 2 + core

    own = [
        pltpu.make_async_copy(context, ctx.at[rows_of(r), :], local_sem.at[0]),
        pltpu.make_async_copy(hidden, hid.at[me], local_sem.at[1]),
        pltpu.make_async_copy(
            residual.at[:, pl.ds(pl.multiple_of(c * width, width), width)],
            res.at[pl.ds(pl.multiple_of(c * res_rows, res_rows), res_rows), :],
            local_sem.at[2],
        ),
    ]
    for copy in own:
        copy.start()

    def w_copy(k):
        part = pl.ds(k * chunk, chunk)
        return pltpu.make_async_copy(weight.at[part, :], w.at[part, :], w_sem.at[k])

    for k in range(CHUNKS):
        w_copy(k).start()
    proj_copy = pltpu.make_async_copy(projector, proj, local_sem.at[3])
    proj_copy.start()

    barrier = pltpu.get_barrier_semaphore()

    up, down, partner = (r + 2, c), (r - 2, c), (r + 1 - 2 * core, c)
    targets = {0: up, 1: down, 2: partner}

    def ctx_copy(pos, k, way, first=False):
        row = row_of(pos)
        cols = pl.ds(k * chunk, chunk)
        there = ctx.at[rows_of(row), cols]
        return pltpu.make_async_remote_copy(
            src_ref=context.at[:, cols] if first else there,
            dst_ref=there,
            send_sem=ctx_send.at[way, pos, k],
            recv_sem=ctx_recv.at[row, k],
            device_id=targets[way],
            device_id_type=MESH,
        )

    def hid_copy(row, col, device, send_sem, first=False):
        slot = row * n_col + col
        return pltpu.make_async_remote_copy(
            src_ref=hidden if first else hid.at[slot],
            dst_ref=hid.at[slot],
            send_sem=send_sem,
            recv_sem=hid_recv.at[slot],
            device_id=device,
            device_id_type=MESH,
        )

    def hid_way(pos, way, first=False):
        return hid_copy(row_of(pos), c, targets[way], hid_chain.at[way, pos], first)

    def hid_side(pos, i, first=False):
        return hid_copy(row_of(pos), c, (r, (c + 1 + i) % n_col), hid_col.at[i, pos], first)

    def hid_cross(pos, i):
        col = (c + 1 + i) % n_col
        return hid_copy(row_of(pos), col, partner, hid_partner.at[i, pos])

    def res_copy(i):
        j = (c + 1 + i) % n_col
        return pltpu.make_async_remote_copy(
            src_ref=residual.at[:, pl.ds(pl.multiple_of(j * width, width), width)],
            dst_ref=res.at[pl.ds(pl.multiple_of(c * res_rows, res_rows), res_rows), :],
            send_sem=col_send.at[0, i],
            recv_sem=col_recv.at[0, c],
            device_id=(r, j),
            device_id_type=MESH,
        )

    has_up, has_down = p < chips - 1, p > 0

    def greet(device):
        pl.semaphore_signal(barrier, inc=1, device_id=device, device_id_type=MESH)

    @pl.when(has_up)
    def _():
        greet(up)

    @pl.when(has_down)
    def _():
        greet(down)

    greet(partner)
    for i in range(n_col - 1):
        greet((r, (c + 1 + i) % n_col))
    peers = n_col + has_up.astype(jnp.int32) + has_down.astype(jnp.int32)
    pl.semaphore_wait(barrier, peers)

    def each_way(guard_up, guard_down, fn):
        @pl.when(guard_up)
        def _():
            fn(0)

        @pl.when(guard_down)
        def _():
            fn(1)

    def own_chunk(k):
        each_way(has_up, has_down, lambda way: ctx_copy(p, k, way, True).start())
        ctx_copy(p, k, 2, True).start()

    for k in range(AHEAD):
        own_chunk(k)
    for i in range(n_col - 1):
        hid_side(p, i, True).start()
        res_copy(i).start()
    hid_way(p, 2, True).start()

    def arrive_hid(pos, way, onward):
        hid_way(pos, way).wait_recv()

        @pl.when(onward)
        def _():
            hid_way(pos, way).start()

        hid_way(pos, 2).start()
        for i in range(n_col - 1):
            hid_side(pos, i).start()

    def arrive_ctx(pos, k, way, onward):
        ctx_copy(pos, k, way).wait_recv()

        @pl.when(onward)
        def _():
            ctx_copy(pos, k, way).start()

        ctx_copy(pos, k, 2).start()

    def both(distance, fn):
        @pl.when(p >= distance)
        def _():
            fn(p - distance, 0, has_up)

        @pl.when(p + distance < chips)
        def _():
            fn(p + distance, 1, has_down)

    own[0].wait()

    def product(j, k):
        cols = pl.ds(pl.multiple_of(j * width, width), width)
        return jnp.dot(
            ctx[:, k * chunk:(k + 1) * chunk],
            w[k * chunk:(k + 1) * chunk, cols],
            preferred_element_type=jnp.float32,
        )

    def part_copy(i):
        j = (c + 1 + i) % n_col
        return pltpu.make_async_remote_copy(
            src_ref=part_out.at[i],
            dst_ref=part_in.at[c],
            send_sem=col_send.at[1, i],
            recv_sem=col_recv.at[1, c],
            device_id=(r, j),
            device_id_type=MESH,
        )

    def multiply(k):
        for pos in range(chips):
            row = pos * 2 + 1 - core
            there = ctx.at[rows_of(row), pl.ds(k * chunk, chunk)]
            pltpu.make_async_remote_copy(
                src_ref=there, dst_ref=there, send_sem=ctx_send.at[2, pos, k],
                recv_sem=ctx_recv.at[row, k], device_id=partner, device_id_type=MESH,
            ).wait_recv()
        w_copy(k).wait()
        if k < CHUNKS - 1:
            def step(j, _, k=k):
                if k == 0:
                    acc[j] = product(j, k)
                else:
                    acc[j] += product(j, k)
                return 0

            lax.fori_loop(0, n_col, step, 0)
        else:
            def last(i, _):
                j = (c + 1 + i) % n_col
                part_out[i] = (acc[j] + product(j, CHUNKS - 1)).astype(jnp.bfloat16)
                part_copy(i).start()
                return 0

            lax.fori_loop(0, n_col - 1, last, 0)
            acc[c] = acc[c] + product(c, CHUNKS - 1)

    for wave in range(1, CHUNKS + chips - 1):
        if wave >= chips:
            multiply(wave - chips)
        for distance in range(1, chips):
            k = wave - distance
            if 0 <= k < CHUNKS:
                both(distance, lambda pos, way, on: arrive_ctx(pos, k, way, on))
            if k == HIDDEN_AT:
                both(distance, arrive_hid)
        if AHEAD - 1 + wave < CHUNKS:
            own_chunk(AHEAD - 1 + wave)
        if wave == max(HIDDEN_AT, 1):
            each_way(has_up, has_down, lambda way: hid_way(p, way, True).start())
    multiply(CHUNKS - 1)

    for pos in range(chips):
        for i in range(n_col - 1):
            j = (c + 1 + i) % n_col
            hid_copy(row_of(pos), j, (r, j), hid_col.at[i, pos]).wait_recv()
            hid_cross(pos, i).start()
    for j in range(student_gain.shape[0]):
        sgain[:, j * LANES:(j + 1) * LANES] = student_gain[j:j + 1, :]
    gain_rows = width // LANES
    for j in range(gain_rows):
        tgain[:, j * LANES:(j + 1) * LANES] = teacher_gain[pl.ds(me * gain_rows + j, 1), :]
    for pos in range(chips):
        for j in range(n_col):
            hid_copy(pos * 2 + 1 - core, j, partner, hid_chain.at[2, pos]).wait_recv()
    own[1].wait()

    group = 8 // hid_rows if hid_rows < 8 else 1

    def widen(s, _):
        wide_rows = pl.ds(pl.multiple_of(s * group * hid_rows, 8), group * hid_rows)
        wide[wide_rows, :] = jnp.concatenate(
            [hid[s * group + i].astype(jnp.float32) for i in range(group)], axis=0
        )
        return 0

    lax.fori_loop(0, devices // group, widen, 0)

    tile = 16

    def normalize(t, _):
        rows = pl.ds(pl.multiple_of(t * tile, tile), tile)
        x = wide[rows, :]
        normed = x * lax.rsqrt(jnp.mean(x * x, axis=1, keepdims=True) + norm_eps)
        wide[rows, :] = normed
        student[rows, :] = (normed * sgain[...]).astype(jnp.bfloat16)
        return 0

    lax.fori_loop(0, tokens // tile, normalize, 0)
    student_copy = pltpu.make_async_copy(student, student_out, local_sem.at[4])
    student_copy.start()
    proj_copy.wait()
    predicted[...] = jnp.dot(student[...], proj[...], preferred_element_type=jnp.float32)

    own[2].wait()
    for i in range(n_col - 1):
        j = (c + 1 + i) % n_col
        pltpu.make_async_remote_copy(
            src_ref=part_out.at[i], dst_ref=part_in.at[j], send_sem=col_send.at[1, i],
            recv_sem=col_recv.at[1, j], device_id=(r, j), device_id_type=MESH,
        ).wait_recv()
        rows = res.at[pl.ds(pl.multiple_of(j * res_rows, res_rows), res_rows), :]
        pltpu.make_async_remote_copy(
            src_ref=rows, dst_ref=rows, send_sem=col_send.at[0, i],
            recv_sem=col_recv.at[0, j], device_id=(r, j), device_id_type=MESH,
        ).wait_recv()
    summed = acc[c] + res[...].astype(jnp.float32)
    for i in range(n_col - 1):
        summed = summed + part_in[(c + 1 + i) % n_col].astype(jnp.float32)
    total[...] = summed
    squares = jnp.sum(summed * summed, axis=1, keepdims=True)
    for b in range(tokens // LANES):
        lanes = slice(b * LANES, (b + 1) * LANES)
        row = to_row(squares[lanes, :])
        sq_out[:, lanes] = row
        sq_in[me, :, lanes] = row

    def to_all(stage, src, dst):
        def copy(i):
            d = (me + 1 + i) % devices
            return pltpu.make_async_remote_copy(
                src_ref=src(d), dst_ref=dst.at[me],
                send_sem=all_send.at[stage], recv_sem=all_recv.at[stage],
                device_id=(d // n_col, d % n_col), device_id_type=MESH,
            )

        def send(i, _):
            copy(i).start()
            return 0

        lax.fori_loop(0, devices - 1, send, 0)

    def wait_all(sem, stage, dst):
        view = dst.at[pl.ds(0, devices - 1)]
        pltpu.make_async_copy(view, view, sem.at[stage]).wait()

    to_all(0, lambda d: sq_out, sq_in)
    wait_all(all_recv, 0, sq_in)
    sums = jnp.sum(sq_in[...], axis=0)
    factor = lax.rsqrt(sums / d_t + norm_eps)
    loss_part = jnp.zeros((1, 1), jnp.float32)
    for b in range(tokens // LANES):
        rows = slice(b * LANES, (b + 1) * LANES)
        target = (total[rows, :] * to_column(factor[:, rows]) * tgain[...]).astype(jnp.bfloat16)
        difference = predicted[rows, :] - target.astype(jnp.float32)
        loss_part = loss_part + jnp.sum(difference * difference, keepdims=True)
        error[rows, :] = (difference * (1.0 / 64.0)).astype(jnp.bfloat16)

    error_copy = pltpu.make_async_copy(error, error_out, local_sem.at[5])
    error_copy.start()

    block = 512

    def gain_step(n, _):
        rows = pl.ds(pl.multiple_of(n * block, block), block)
        grad_normed = lax.dot_general(
            error[...], proj[rows, :], (((1,), (1,)), ((), ())),
            preferred_element_type=jnp.float32,
        )
        part = jnp.sum(grad_normed * wide[:, rows], axis=0, keepdims=True)
        for q in range(block // LANES):
            gp[n * (block // LANES) + q, 0:1, :] = part[:, q * LANES:(q + 1) * LANES]
            gp[n * (block // LANES) + q, 1:2, :] = jnp.broadcast_to(loss_part, (1, LANES))
        return 0

    lax.fori_loop(0, d_s // block, gain_step, 0)
    gp_in[me] = gp[me // repeat]
    to_all(1, lambda d: gp.at[d // repeat], gp_in)
    wait_all(all_recv, 1, gp_in)
    both_sums = jnp.sum(gp_in[...], axis=0)
    gg_out[...] = both_sums[0:1, :]
    gg[me] = both_sums[0:1, :]
    to_all(2, lambda d: gg_out, gg)
    loss_out[...] = both_sums[1:2, :] / (tokens * d_t)
    wait_all(all_recv, 2, gg)
    for j in range(segments):
        gain_out[j:j + 1, :] = gg[j * repeat]

    student_copy.wait()
    error_copy.wait()
    each_way(has_up, has_down, lambda way: hid_way(p, way).wait_send())
    hid_way(p, 2).wait_send()
    for k in range(CHUNKS):
        each_way(has_up, has_down, lambda way: ctx_copy(p, k, way).wait_send())
        ctx_copy(p, k, 2).wait_send()
    for i in range(n_col - 1):
        hid_side(p, i).wait_send()
        res_copy(i).wait_send()
        part_copy(i).wait_send()

    def left(pos, way, onward):
        @pl.when(onward)
        def _():
            hid_way(pos, way).wait_send()
            for k in range(CHUNKS):
                ctx_copy(pos, k, way).wait_send()

        hid_way(pos, 2).wait_send()
        for k in range(CHUNKS):
            ctx_copy(pos, k, 2).wait_send()
        for i in range(n_col - 1):
            hid_side(pos, i).wait_send()

    for distance in range(1, chips):
        both(distance, left)
    for pos in range(chips):
        for i in range(n_col - 1):
            hid_cross(pos, i).wait_send()
    wait_all(all_send, 0, sq_in)
    wait_all(all_send, 1, gp_in)
    wait_all(all_send, 2, gg)


def per_device(
    n_row, n_col,
    context, out_weight, residual, teacher_gain, student_hidden, student_gain, projector,
):
    devices = n_row * n_col
    chips = n_row // 2
    tokens = context.shape[0] * n_row
    d_s, width = projector.shape
    segments = min(devices, d_s // LANES)
    f32, bf16 = jnp.float32, jnp.bfloat16
    anywhere = pl.BlockSpec(memory_space=pl.ANY)
    vmem = pl.BlockSpec(memory_space=pltpu.VMEM)
    dma = pltpu.SemaphoreType.DMA
    student_all, error_term, grad_gain, loss = pl.pallas_call(
        functools.partial(body, n_row, n_col),
        out_shape=(
            jax.ShapeDtypeStruct((tokens, d_s), bf16),
            jax.ShapeDtypeStruct((tokens, width), bf16),
            jax.ShapeDtypeStruct((segments, LANES), f32),
            jax.ShapeDtypeStruct((1, LANES), f32),
        ),
        in_specs=[anywhere, anywhere, anywhere, vmem, anywhere, vmem, anywhere],
        out_specs=(anywhere, anywhere, vmem, vmem),
        scratch_shapes=[
            pltpu.VMEM((tokens, d_s), bf16),
            pltpu.VMEM((tokens, width), bf16),
            pltpu.VMEM((tokens, context.shape[1]), bf16),
            pltpu.VMEM(out_weight.shape, bf16),
            pltpu.VMEM((d_s, width), bf16),
            pltpu.VMEM((n_col, tokens, width), f32),
            pltpu.VMEM((n_col - 1, tokens, width), bf16),
            pltpu.VMEM((n_col, tokens, width), bf16),
            pltpu.VMEM((tokens, width), bf16),
            pltpu.VMEM((devices,) + student_hidden.shape, bf16),
            pltpu.VMEM((tokens, d_s), f32),
            pltpu.VMEM((1, d_s), f32),
            pltpu.VMEM((1, width), f32),
            pltpu.VMEM((tokens, width), f32),
            pltpu.VMEM((tokens, width), f32),
            pltpu.VMEM((1, tokens), f32),
            pltpu.VMEM((devices, 1, tokens), f32),
            pltpu.VMEM((d_s // LANES, 2, LANES), f32),
            pltpu.VMEM((devices, 2, LANES), f32),
            pltpu.VMEM((1, LANES), f32),
            pltpu.VMEM((devices, 1, LANES), f32),
            dma((6,)),
            dma((CHUNKS,)),
            dma((3, chips, CHUNKS)),
            dma((n_row, CHUNKS)),
            dma((3, chips)),
            dma((n_col, chips)),
            dma((n_col, chips)),
            dma((devices,)),
            dma((2, n_col)),
            dma((2, n_col)),
            dma((3,)),
            dma((3,)),
        ],
        compiler_params=pltpu.CompilerParams(
            collective_id=0, has_side_effects=True, vmem_limit_bytes=67_000_000
        ),
    )(
        context, out_weight, residual, teacher_gain.reshape(-1, LANES), student_hidden,
        student_gain.reshape(-1, LANES), projector,
    )
    grad_proj = lax.dot_general(
        student_all, error_term, (((0,), (0,)), ((), ())), preferred_element_type=f32
    )
    return (grad_proj, grad_gain.reshape(-1), loss[0, 0])


def solution(mesh):
    placed = (
        P("row", "col"),
        P("col", "row"),
        P("col", "row"),
        P(),
        P(("row", "col"), None),
        P(),
        P(None, ("row", "col")),
    )
    return jax.shard_map(
        functools.partial(per_device, mesh.shape["row"], mesh.shape["col"]),
        mesh=mesh,
        in_specs=placed,
        out_specs=(P(None, ("row", "col")), P(), P()),
        check_vma=False,
    )
```
